32 devices in a mesh: layer: 4 (over y, x), col: 8 (over z, core).
Axes of the slice: x: 2, y: 2, z: 4, core: 2. Of those that a mesh axis runs over, the one named last changes fastest.
Arguments:
- inputs: bfloat16 [4, 128, 4096], replicated, may hold values from -6 to 6
- w_input: bfloat16 [4, 4096, 4, 4096], P('layer', None, None, 'col'), may hold values from -0.09375 to 0.09375
- w_recur: bfloat16 [4, 4096, 4, 4096], P('layer', None, None, 'col'), may hold values from -0.09375 to 0.09375
- bias: float32 [4, 4, 4096], P('layer', None, 'col'), may hold values from -1 to 2
- h_start: bfloat16 [4, 128, 4096], P('layer', None, 'col'), may hold values from -3 to 3
- c_start: float32 [4, 128, 4096], P('layer', None, 'col'), may hold values from -6 to 6
Outputs:
- hidden_seq: bfloat16 [4, 4, 128, 4096], P('layer', None, None, 'col')
- cell_final: float32 [4, 128, 4096], P('layer', None, 'col')
The draws below stay inside these ranges and needn't reach their ends.
All inputs are finite; a program needn't handle non-finite values.
Results may differ from the reference program's by a relative error of at most 0.0024.
Values may be sent and summed in bfloat16 or wider, within the bound.
A program may use at most 128 MiB of HBM per device.

```python
import jax
import jax.numpy as jnp
from jax import lax

H = 4096
BATCH = 128
TSTEPS = 4
LAYERS = 4


def steps_of(rng, extent, cuts, smallest, high):
    loudness, own = 1.0, jax.random.fold_in(rng, 6)
    for dim, shards_of in cuts:
        heights = jnp.exp(jax.random.uniform(jax.random.fold_in(own, dim), (shards_of,), jnp.float32, smallest / len(cuts), high / len(cuts)))
        loudness = loudness * jnp.repeat(heights, extent[dim] // shards_of).reshape([-1 if axis == dim else 1 for axis in range(len(extent))])
    return loudness


def scatter_about(own_key, dims, width, limit, split=(), held_as=jnp.bfloat16):
    entries = jax.random.normal(own_key, dims, jnp.float32) * width
    if len(split) > 0:
        entries = steps_of(own_key, dims, split, -0.22, 0.18) * entries
    return jnp.clip(entries, min=-limit, max=limit).astype(held_as)


def setup_inputs(seed: int = 0) -> dict:
    seeds = jax.random.split(jax.random.key(seed), 7)
    inputs = scatter_about(seeds[0], (TSTEPS, BATCH, H), 1.0, 6.0)
    w_input = scatter_about(seeds[1], (LAYERS, H, 4, H), H ** -0.5, 0.09375, ((0, 4), (3, 8)))
    w_recur = scatter_about(seeds[2], (LAYERS, H, 4, H), H ** -0.5, 0.09375, ((0, 4), (3, 8)))
    bias = jnp.clip(-1.0 + 3.0 * jax.random.uniform(seeds[3], (LAYERS, 4, H), jnp.float32) ** steps_of(seeds[3], (LAYERS, 4, H), ((0, 4), (2, 8)), -0.2, 0.2), -1.0, 2.0)
    h_start = scatter_about(seeds[4], (LAYERS, BATCH, H), 0.5, 3.0, ((0, 4), (2, 8)))
    c_start = scatter_about(seeds[5], (LAYERS, BATCH, H), 1.0, 6.0, ((0, 4), (2, 8)), jnp.float32)
    return {"inputs": inputs, "w_input": w_input, "w_recur": w_recur, "bias": bias, "h_start": h_start, "c_start": c_start}


def reference(inputs, w_input, w_recur, bias, h_start, c_start):
    layers = w_input.shape[0]
    source = inputs
    hidden_all = []
    cell_all = []
    for layer in range(layers):
        weight_in = w_input[layer].reshape(H, 4 * H)
        weight_rec = w_recur[layer].reshape(H, 4 * H)
        offset = bias[layer].reshape(4 * H)
        projected = jnp.dot(source.reshape(TSTEPS * BATCH, H), weight_in, preferred_element_type=jnp.float32) + offset
        projected = projected.reshape(TSTEPS, BATCH, 4 * H)

        def advance(carry, z_in, weight_rec=weight_rec):
            hidden, cell = carry
            gates = z_in + jnp.dot(hidden, weight_rec, preferred_element_type=jnp.float32)
            gates = gates.reshape(BATCH, 4, H)
            cell_new = jax.nn.sigmoid(gates[:, 1]) * cell + jax.nn.sigmoid(gates[:, 0]) * jnp.tanh(gates[:, 2])
            hidden_new = (jax.nn.sigmoid(gates[:, 3]) * jnp.tanh(cell_new)).astype(jnp.bfloat16)
            return (hidden_new, cell_new), hidden_new

        (hidden_last, cell_last), outputs = lax.scan(advance, (h_start[layer], c_start[layer]), projected)
        hidden_all.append(outputs)
        cell_all.append(cell_last)
        source = outputs
    return jnp.stack(hidden_all), jnp.stack(cell_all)
```

```python
import functools

import jax
import jax.numpy as jnp
from jax import lax
from jax.experimental import pallas as pl
from jax.experimental.pallas import tpu as pltpu
from jax.sharding import PartitionSpec as P

MESH = pl.DeviceIdType.MESH
LEFT, RIGHT, SIBLING, NEXT = range(4)


def kernel(
    groups, devices, inputs_ref, w_in_ref, w_rec_ref, bias_ref, h_start_ref, c_start_ref,
    hidden_ref, cell_ref,
    weights, held, gates, recv_sem, send_sem, pass_sem, weight_sem,
):
    steps, batch, local = hidden_ref.shape
    chips = devices // 2
    layer = lax.axis_index("layer")
    me = lax.axis_index("col")
    chip, core = me // 2, lax.rem(me, 2)
    sibling = 2 * chip + 1 - core
    has_left, has_right = chip > 0, chip < chips - 1
    has_prev, has_next = layer > 0, layer < groups - 1

    partners = (
        (has_left, layer, me - 2),
        (has_right, layer, me + 2),
        (None, layer, sibling),
        (has_next, layer + 1, me),
        (has_prev, layer - 1, me),
    )

    def when(condition, action):
        if condition is None:
            action()
        else:
            pl.when(condition)(action)

    def weight_copy(kind, block):
        rows = pl.ds(pl.multiple_of(block * local, local), local)
        source = w_rec_ref if kind == 0 else w_in_ref
        return pltpu.make_async_copy(
            source.at[rows, :], weights.at[kind, rows, :], weight_sem.at[kind, block]
        )

    def input_copy(step, block):
        columns = pl.ds(pl.multiple_of(block * local, local), local)
        return pltpu.make_async_copy(
            inputs_ref.at[step, :, columns], held.at[1, step, block], recv_sem.at[1, step, block]
        )

    start_copy = pltpu.make_async_copy(h_start_ref, held.at[0, 0, me], recv_sem.at[0, 0, me])
    start_copy.start()

    @pl.loop(0, devices)
    def _(block):
        weight_copy(0, block).start()

    @pl.when(layer == 0)
    def _():
        @pl.loop(0, devices)
        def _(block):
            input_copy(0, block).start()

    @pl.loop(0, devices)
    def _(block):
        weight_copy(1, block).start()

    @pl.when(layer == 0)
    def _():
        @pl.loop(1, steps)
        def _(step):
            @pl.loop(0, devices)
            def _(block):
                input_copy(step, block).start()

    barrier = pltpu.get_barrier_semaphore()
    expected = jnp.int32(0)
    for condition, there, col in partners:
        expected = expected + (1 if condition is None else condition.astype(jnp.int32))

        def greet(there=there, col=col):
            pl.semaphore_signal(barrier, inc=1, device_id=(there, col), device_id_type=MESH)

        when(condition, greet)
    pl.semaphore_wait(barrier, expected)

    def hidden_copy(slot, block, way):
        _, there, col = partners[way]
        target = held.at[1, slot - 1, block] if way == NEXT else held.at[0, slot, block]
        arrival = recv_sem.at[1, slot - 1, block] if way == NEXT else recv_sem.at[0, slot, block]
        return pltpu.make_async_remote_copy(
            src_ref=held.at[0, slot, block],
            dst_ref=target,
            send_sem=send_sem.at[slot, block // 2, way],
            recv_sem=arrival,
            device_id=(there, col),
            device_id_type=MESH,
        )

    def source_copy(slot, block):
        return pltpu.make_async_remote_copy(
            src_ref=held.at[1, slot, block],
            dst_ref=held.at[1, slot, block],
            send_sem=pass_sem.at[slot, block // 2],
            recv_sem=recv_sem.at[1, slot, block],
            device_id=(layer, sibling),
            device_id_type=MESH,
        )

    def arrived(kind, slot, block):
        pltpu.make_async_copy(
            held.at[kind, slot, block], held.at[kind, slot, block], recv_sem.at[kind, slot, block]
        ).wait()

    def ways_of(slot, owner):
        return (
            (LEFT, jnp.logical_and(has_left, owner >= chip)),
            (RIGHT, jnp.logical_and(has_right, owner <= chip)),
            (SIBLING, slot < steps),
            (NEXT, jnp.logical_and(has_next, slot >= 1)),
        )

    start_copy.wait()
    cell_ref[...] = c_start_ref[...]

    def multiply(kind, slot, block):
        rows = pl.ds(pl.multiple_of(block * local, local), local)
        gates[...] += jnp.dot(
            held[kind, slot, block], weights[kind, rows, :], preferred_element_type=jnp.float32
        )

    def turn(slot, _):
        compute = slot < steps
        first = slot == 0

        @pl.when(compute)
        def _():
            gates[...] = jnp.broadcast_to(bias_ref[...], gates.shape)

        def event(index, _):
            place = jnp.where(first, lax.rem(index, 4 * chips), index)
            kind = jnp.where(first, index // (4 * chips), lax.rem(index // 2, 2))
            away = jnp.where(first, place // 4, place // 8)
            passed = jnp.where(first, lax.rem(place // 2, 2), lax.rem(place // 4, 2))
            upward = lax.rem(index, 2)
            owner = jnp.where(upward == 0, chip - away, chip + away)
            block = 2 * owner + jnp.where(passed == 0, core, 1 - core)
            valid = jnp.logical_and(owner >= 0, owner < chips)
            valid = jnp.logical_and(valid, jnp.logical_or(away > 0, upward == 0))
            valid = jnp.logical_and(
                valid, jnp.logical_or(compute, jnp.logical_and(kind == 0, passed == 0))
            )

            @pl.when(valid)
            def _():
                mine = jnp.logical_and(kind == 0, jnp.logical_and(away == 0, passed == 0))

                @pl.when(jnp.logical_not(mine))
                def _():
                    arrived(kind, slot, block)

                @pl.when(jnp.logical_and(kind == 0, passed == 0))
                def _():
                    for way, condition in ways_of(slot, owner):
                        pl.when(condition)(lambda way=way: hidden_copy(slot, block, way).start())

                @pl.when(jnp.logical_and(kind == 1, jnp.logical_and(passed == 0, has_prev)))
                def _():
                    source_copy(slot, block).start()

                for which in range(2):
                    @pl.when(jnp.logical_and(first, kind == which))
                    def _():
                        weight_copy(which, block).wait()

                @pl.when(compute)
                def _():
                    multiply(kind, slot, block)

            return 0

        lax.fori_loop(0, 8 * chips, event, 0)

        @pl.when(compute)
        def _():
            part = 16

            def rows_of(index, _):
                rows = pl.ds(pl.multiple_of(index * part, part), part)

                def gate(which):
                    return gates[rows, which * local : (which + 1) * local]

                cell = jax.nn.sigmoid(gate(1)) * cell_ref[rows, :] + jax.nn.sigmoid(
                    gate(0)
                ) * jnp.tanh(gate(2))
                cell_ref[rows, :] = cell
                hidden = (jax.nn.sigmoid(gate(3)) * jnp.tanh(cell)).astype(jnp.bfloat16)
                hidden_ref[slot, rows, :] = hidden
                held[0, slot + 1, me, rows, :] = hidden
                return 0

            lax.fori_loop(0, batch // part, rows_of, 0)

        return 0

    turns = jnp.where(has_next, steps + 1, steps)
    lax.fori_loop(0, turns, turn, 0)

    def drain(slot, _):
        def drain_block(owner, _):
            block = 2 * owner + core
            for way, condition in ways_of(slot, owner):
                pl.when(condition)(lambda way=way: hidden_copy(slot, block, way).wait_send())

            @pl.when(jnp.logical_and(has_prev, slot < steps))
            def _():
                source_copy(slot, block).wait_send()

            return 0

        return lax.fori_loop(0, chips, drain_block, 0)

    lax.fori_loop(0, turns, drain, 0)


def body(inputs, w_input, w_recur, bias, h_start, c_start):
    steps, batch, width = inputs.shape
    local = w_input.shape[3]
    groups = lax.axis_size("layer")
    devices = lax.axis_size("col")
    vmem = pl.BlockSpec(memory_space=pltpu.VMEM)
    anywhere = pl.BlockSpec(memory_space=pl.ANY)
    hidden, cell = pl.pallas_call(
        functools.partial(kernel, groups, devices),
        out_shape=(
            jax.ShapeDtypeStruct((steps, batch, local), jnp.bfloat16),
            jax.ShapeDtypeStruct((batch, local), jnp.float32),
        ),
        in_specs=[anywhere, anywhere, anywhere, vmem, anywhere, vmem],
        out_specs=(vmem, vmem),
        scratch_shapes=[
            pltpu.VMEM((2, width, 4 * local), jnp.bfloat16),
            pltpu.VMEM((2, steps + 1, devices, batch, local), jnp.bfloat16),
            pltpu.VMEM((batch, 4 * local), jnp.float32),
            pltpu.SemaphoreType.DMA((2, steps + 1, devices)),
            pltpu.SemaphoreType.DMA((steps + 1, devices // 2, 4)),
            pltpu.SemaphoreType.DMA((steps, devices // 2)),
            pltpu.SemaphoreType.DMA((2, devices)),
        ],
        compiler_params=pltpu.CompilerParams(
            collective_id=0, has_side_effects=True, vmem_limit_bytes=60 * 1024 * 1024
        ),
    )(
        inputs,
        w_input[0].reshape(width, 4 * local),
        w_recur[0].reshape(width, 4 * local),
        bias[0].reshape(1, 4 * local),
        h_start[0],
        c_start[0],
    )
    return (hidden[None], cell[None])


def solution(mesh):
    in_specs = (
        P(),
        P("layer", None, None, "col"),
        P("layer", None, None, "col"),
        P("layer", None, "col"),
        P("layer", None, "col"),
        P("layer", None, "col"),
    )
    out_specs = (P("layer", None, None, "col"), P("layer", None, "col"))
    return jax.shard_map(body, mesh=mesh, in_specs=in_specs, out_specs=out_specs, check_vma=False)
```

```python
import functools

import jax
import jax.numpy as jnp
from jax import lax
from jax.experimental import pallas as pl
from jax.experimental.pallas import tpu as pltpu
from jax.sharding import PartitionSpec as P

MESH = pl.DeviceIdType.MESH
LEFT, RIGHT, SIBLING, NEXT = range(4)


def kernel(
    groups, devices, cuts, inputs_ref, w_in_ref, w_rec_ref, bias_ref, h_start_ref, c_start_ref,
    hidden_ref, cell_ref,
    weights, raw, held, gates, recv_sem, send_sem, pass_sem, raw_sem,
):
    steps, batch, local = hidden_ref.shape
    piece = local // cuts
    chips = devices // 2
    chunks, depth = 2 * devices, raw.shape[0]
    layer = lax.axis_index("layer")
    me = lax.axis_index("col")
    chip, core = me // 2, lax.rem(me, 2)
    sibling = 2 * chip + 1 - core
    has_left, has_right = chip > 0, chip < chips - 1
    has_prev, has_next = layer > 0, layer < groups - 1

    partners = (
        (has_left, layer, me - 2),
        (has_right, layer, me + 2),
        (None, layer, sibling),
        (has_next, layer + 1, me),
        (has_prev, layer - 1, me),
    )

    def when(condition, action):
        if condition is None:
            action()
        else:
            pl.when(condition)(action)

    def raw_copy(source, chunk):
        rows = pl.ds(pl.multiple_of(lax.rem(chunk, devices) * local, local), local)
        slot = lax.rem(chunk, depth)
        return pltpu.make_async_copy(source.at[rows], raw.at[slot], raw_sem.at[slot])

    def raw_start(chunk):
        pl.when(chunk < devices)(lambda: raw_copy(w_rec_ref, chunk).start())
        pl.when(jnp.logical_and(chunk >= devices, chunk < chunks))(
            lambda: raw_copy(w_in_ref, chunk).start()
        )

    def unpack(chunk):
        slot = lax.rem(chunk, depth)
        raw_copy(w_rec_ref, chunk).wait()
        kind, base = chunk // devices, lax.rem(chunk, devices) * local
        part = min(64, local)

        @pl.loop(0, local // part)
        def _(index):
            inner = pl.multiple_of(index * part, part)
            rows = pl.ds(pl.multiple_of(base + inner, part), part)
            weights[kind, rows, :] = raw[slot, pl.ds(inner, part)].reshape(part, 4 * local)

        raw_start(chunk + depth)

    def input_copy(step, block):
        columns = pl.ds(pl.multiple_of(block * piece, piece), piece)
        return pltpu.make_async_copy(
            inputs_ref.at[step, :, columns], held.at[1, step, block], recv_sem.at[1, step, block]
        )

    def start_copy(part):
        columns = slice(part * piece, (part + 1) * piece)
        block = me * cuts + part
        return pltpu.make_async_copy(
            h_start_ref.at[:, columns], held.at[0, 0, block], recv_sem.at[0, 0, block]
        )

    for part in range(cuts):
        start_copy(part).start()

    @pl.loop(0, depth)
    def _(chunk):
        raw_start(chunk)

    @pl.when(layer == 0)
    def _():
        @pl.loop(0, steps)
        def _(step):
            @pl.loop(0, devices * cuts)
            def _(block):
                input_copy(step, block).start()

    barrier = pltpu.get_barrier_semaphore()
    expected = jnp.int32(0)
    for condition, there, col in partners:
        expected = expected + (1 if condition is None else condition.astype(jnp.int32))

        def greet(there=there, col=col):
            pl.semaphore_signal(barrier, inc=1, device_id=(there, col), device_id_type=MESH)

        when(condition, greet)
    pl.semaphore_wait(barrier, expected)

    def hidden_copy(slot, block, way):
        _, there, col = partners[way]
        target = held.at[1, slot - 1, block] if way == NEXT else held.at[0, slot, block]
        arrival = recv_sem.at[1, slot - 1, block] if way == NEXT else recv_sem.at[0, slot, block]
        return pltpu.make_async_remote_copy(
            src_ref=held.at[0, slot, block],
            dst_ref=target,
            send_sem=send_sem.at[slot, place_of(block), way],
            recv_sem=arrival,
            device_id=(there, col),
            device_id_type=MESH,
        )

    def place_of(block):
        return block // (2 * cuts) * cuts + lax.rem(block, cuts)

    def source_copy(slot, block):
        return pltpu.make_async_remote_copy(
            src_ref=held.at[1, slot, block],
            dst_ref=held.at[1, slot, block],
            send_sem=pass_sem.at[slot, place_of(block)],
            recv_sem=recv_sem.at[1, slot, block],
            device_id=(layer, sibling),
            device_id_type=MESH,
        )

    def arrived(kind, slot, block):
        pltpu.make_async_copy(
            held.at[kind, slot, block], held.at[kind, slot, block], recv_sem.at[kind, slot, block]
        ).wait()

    def ways_of(slot, owner):
        wanted = jnp.logical_or(slot < steps, has_next)
        return (
            (LEFT, jnp.logical_and(wanted, jnp.logical_and(has_left, owner >= chip))),
            (RIGHT, jnp.logical_and(wanted, jnp.logical_and(has_right, owner <= chip))),
            (NEXT, jnp.logical_and(has_next, slot >= 1)),
            (SIBLING, slot < steps),
        )

    def send_hidden(slot, owner, block):
        for way, condition in ways_of(slot, owner):
            pl.when(condition)(lambda way=way: hidden_copy(slot, block, way).start())

    cell_ref[...] = c_start_ref[...]

    for part in range(cuts):
        start_copy(part).wait()
        send_hidden(0, chip, me * cuts + part)

    def opening(index, _):
        away, passed, upward = index // 4, lax.rem(index // 2, 2), lax.rem(index, 2)
        owner = jnp.where(upward == 0, chip - away, chip + away)
        col = 2 * owner + jnp.where(passed == 0, core, 1 - core)
        valid = jnp.logical_and(owner >= 0, owner < chips)
        valid = jnp.logical_and(valid, jnp.logical_or(away > 0, upward == 0))
        valid = jnp.logical_and(valid, jnp.logical_or(away > 0, passed == 1))

        @pl.when(valid)
        def _():
            for part in range(cuts):
                block = col * cuts + part
                arrived(0, 0, block)
                pl.when(passed == 0)(lambda block=block: send_hidden(0, owner, block))

        unpack(index)
        return 0

    lax.fori_loop(0, chunks, opening, 0)

    def multiply(kind, slot, block):
        rows = pl.ds(pl.multiple_of(block * piece, piece), piece)
        gates[...] += jnp.dot(
            held[kind, slot, block], weights[kind, rows, :], preferred_element_type=jnp.float32
        )

    def turn(slot, _):
        compute = slot < steps
        first = slot == 0
        half, whole = 4 * cuts * chips, 8 * cuts

        @pl.when(compute)
        def _():
            gates[...] = jnp.broadcast_to(bias_ref[...], gates.shape)

        def event(index, _):
            place = jnp.where(first, lax.rem(index, half), index)
            away = jnp.where(first, place // (4 * cuts), place // whole)
            place = jnp.where(first, lax.rem(place, 4 * cuts), lax.rem(place, whole))
            kind = jnp.where(first, index // half, lax.rem(place // 2, 2))
            passed = jnp.where(first, place // (2 * cuts), place // (4 * cuts))
            part = jnp.where(first, lax.rem(place // 2, cuts), lax.rem(place // 4, cuts))
            upward = lax.rem(index, 2)
            owner = jnp.where(upward == 0, chip - away, chip + away)
            block = (2 * owner + jnp.where(passed == 0, core, 1 - core)) * cuts + part
            valid = jnp.logical_and(owner >= 0, owner < chips)
            valid = jnp.logical_and(valid, jnp.logical_or(away > 0, upward == 0))
            valid = jnp.logical_and(
                valid, jnp.logical_or(compute, jnp.logical_and(kind == 0, passed == 0))
            )

            @pl.when(valid)
            def _():
                mine = jnp.logical_and(away == 0, passed == 0)
                here = jnp.logical_and(kind == 0, jnp.logical_or(mine, first))

                @pl.when(jnp.logical_not(here))
                def _():
                    arrived(kind, slot, block)

                    @pl.when(jnp.logical_and(kind == 0, passed == 0))
                    def _():
                        send_hidden(slot, owner, block)

                    @pl.when(jnp.logical_and(kind == 1, jnp.logical_and(passed == 0, has_prev)))
                    def _():
                        source_copy(slot, block).start()

                @pl.when(compute)
                def _():
                    multiply(kind, slot, block)

            return 0

        lax.fori_loop(0, 8 * cuts * chips, event, 0)

        @pl.when(compute)
        def _():
            height = 32
            for part in range(cuts):
                columns = slice(part * piece, (part + 1) * piece)

                def rows_of(index, _):
                    rows = pl.ds(pl.multiple_of(index * height, height), height)

                    def gate(which):
                        return gates[
                            rows, which * local + part * piece : which * local + (part + 1) * piece
                        ]

                    cell = jax.nn.sigmoid(gate(1)) * cell_ref[rows, columns] + jax.nn.sigmoid(
                        gate(0)
                    ) * jnp.tanh(gate(2))
                    cell_ref[rows, columns] = cell
                    hidden = (jax.nn.sigmoid(gate(3)) * jnp.tanh(cell)).astype(jnp.bfloat16)
                    hidden_ref[slot, rows, columns] = hidden
                    held[0, slot + 1, me * cuts + part, rows, :] = hidden
                    return 0

                lax.fori_loop(0, batch // height, rows_of, 0)
                send_hidden(slot + 1, chip, me * cuts + part)

        return 0

    turns = jnp.where(has_next, steps + 1, steps)
    lax.fori_loop(0, turns, turn, 0)

    def drain(slot, _):
        def drain_block(index, _):
            owner, part = index // cuts, lax.rem(index, cuts)
            block = (2 * owner + core) * cuts + part
            for way, condition in ways_of(slot, owner):
                pl.when(condition)(lambda way=way: hidden_copy(slot, block, way).wait_send())

            @pl.when(jnp.logical_and(has_prev, slot < steps))
            def _():
                source_copy(slot, block).wait_send()

            return 0

        return lax.fori_loop(0, chips * cuts, drain_block, 0)

    lax.fori_loop(0, turns, drain, 0)


def body(inputs, w_input, w_recur, bias, h_start, c_start):
    steps, batch, width = inputs.shape
    local = w_input.shape[3]
    groups = lax.axis_size("layer")
    devices = lax.axis_size("col")
    cuts = 2 if local % 512 == 0 else 1
    vmem = pl.BlockSpec(memory_space=pltpu.VMEM)
    anywhere = pl.BlockSpec(memory_space=pl.ANY)
    hidden, cell = pl.pallas_call(
        functools.partial(kernel, groups, devices, cuts),
        out_shape=(
            jax.ShapeDtypeStruct((steps, batch, local), jnp.bfloat16),
            jax.ShapeDtypeStruct((batch, local), jnp.float32),
        ),
        in_specs=[anywhere, anywhere, anywhere, vmem, anywhere, vmem],
        out_specs=(vmem, vmem),
        scratch_shapes=[
            pltpu.VMEM((2, width, 4 * local), jnp.bfloat16),
            pltpu.VMEM((4, local, 4, local), jnp.bfloat16),
            pltpu.VMEM((2, steps + 1, devices * cuts, batch, local // cuts), jnp.bfloat16),
            pltpu.VMEM((batch, 4 * local), jnp.float32),
            pltpu.SemaphoreType.DMA((2, steps + 1, devices * cuts)),
            pltpu.SemaphoreType.DMA((steps + 1, devices // 2 * cuts, 4)),
            pltpu.SemaphoreType.DMA((steps, devices // 2 * cuts)),
            pltpu.SemaphoreType.DMA((4,)),
        ],
        compiler_params=pltpu.CompilerParams(
            collective_id=0, has_side_effects=True, vmem_limit_bytes=60 * 1024 * 1024
        ),
    )(
        inputs,
        w_input[0],
        w_recur[0],
        bias[0].reshape(1, 4 * local),
        h_start[0],
        c_start[0],
    )
    return (hidden[None], cell[None])


def solution(mesh):
    in_specs = (
        P(),
        P("layer", None, None, "col"),
        P("layer", None, None, "col"),
        P("layer", None, "col"),
        P("layer", None, "col"),
        P("layer", None, "col"),
    )
    out_specs = (P("layer", None, None, "col"), P("layer", None, "col"))
    return jax.shard_map(body, mesh=mesh, in_specs=in_specs, out_specs=out_specs, check_vma=False)
```

```python
import functools

import jax
import jax.numpy as jnp
from jax import lax
from jax.experimental import pallas as pl
from jax.experimental.pallas import tpu as pltpu
from jax.sharding import PartitionSpec as P

MESH = pl.DeviceIdType.MESH
LEFT, RIGHT, SIBLING, NEXT = range(4)


def kernel(
    groups, devices, cuts, inputs_ref, w_in_ref, w_rec_ref, bias_ref, h_start_ref, c_start_ref,
    hidden_ref, cell_ref,
    weights, raw, held, gates, recv_sem, send_sem, pass_sem, raw_sem,
):
    steps, batch, local = hidden_ref.shape
    piece = local // cuts
    chips = devices // 2
    chunks, depth = 2 * devices, raw.shape[0]
    layer = lax.axis_index("layer")
    me = lax.axis_index("col")
    chip, core = me // 2, lax.rem(me, 2)
    sibling = 2 * chip + 1 - core
    has_left, has_right = chip > 0, chip < chips - 1
    has_prev, has_next = layer > 0, layer < groups - 1

    partners = (
        (has_left, layer, me - 2),
        (has_right, layer, me + 2),
        (None, layer, sibling),
        (has_next, layer + 1, me),
        (has_prev, layer - 1, me),
    )

    def when(condition, action):
        if condition is None:
            action()
        else:
            pl.when(condition)(action)

    def raw_copy(source, chunk):
        rows = pl.ds(pl.multiple_of(lax.rem(chunk, devices) * local, local), local)
        slot = lax.rem(chunk, depth)
        return pltpu.make_async_copy(source.at[rows], raw.at[slot], raw_sem.at[slot])

    def raw_start(chunk):
        pl.when(chunk < devices)(lambda: raw_copy(w_in_ref, chunk).start())
        pl.when(jnp.logical_and(chunk >= devices, chunk < chunks))(
            lambda: raw_copy(w_rec_ref, chunk).start()
        )

    def unpack(chunk):
        slot = lax.rem(chunk, depth)
        raw_copy(w_rec_ref, chunk).wait()
        kind, base = 1 - chunk // devices, lax.rem(chunk, devices) * local
        part = min(64, local)

        @pl.loop(0, local // part)
        def _(index):
            inner = pl.multiple_of(index * part, part)
            rows = pl.ds(pl.multiple_of(base + inner, part), part)
            weights[kind, rows, :] = raw[slot, pl.ds(inner, part)].reshape(part, 4 * local)

        raw_start(chunk + depth)

    def input_copy(step, block):
        columns = pl.ds(pl.multiple_of(block * piece, piece), piece)
        return pltpu.make_async_copy(
            inputs_ref.at[step, :, columns], held.at[1, step, block], recv_sem.at[1, step, block]
        )

    def start_copy(part):
        columns = slice(part * piece, (part + 1) * piece)
        block = me * cuts + part
        return pltpu.make_async_copy(
            h_start_ref.at[:, columns], held.at[0, 0, block], recv_sem.at[0, 0, block]
        )

    for part in range(cuts):
        start_copy(part).start()

    @pl.loop(0, depth)
    def _(chunk):
        raw_start(chunk)

    @pl.when(layer == 0)
    def _():
        @pl.loop(0, steps)
        def _(step):
            @pl.loop(0, devices * cuts)
            def _(block):
                input_copy(step, block).start()

    barrier = pltpu.get_barrier_semaphore()
    expected = jnp.int32(0)
    for condition, there, col in partners:
        expected = expected + (1 if condition is None else condition.astype(jnp.int32))

        def greet(there=there, col=col):
            pl.semaphore_signal(barrier, inc=1, device_id=(there, col), device_id_type=MESH)

        when(condition, greet)
    pl.semaphore_wait(barrier, expected)

    def hidden_copy(slot, block, way):
        _, there, col = partners[way]
        target = held.at[1, slot - 1, block] if way == NEXT else held.at[0, slot, block]
        arrival = recv_sem.at[1, slot - 1, block] if way == NEXT else recv_sem.at[0, slot, block]
        return pltpu.make_async_remote_copy(
            src_ref=held.at[0, slot, block],
            dst_ref=target,
            send_sem=send_sem.at[slot, place_of(block), way],
            recv_sem=arrival,
            device_id=(there, col),
            device_id_type=MESH,
        )

    def place_of(block):
        return block // (2 * cuts) * cuts + lax.rem(block, cuts)

    def source_copy(slot, block):
        return pltpu.make_async_remote_copy(
            src_ref=held.at[1, slot, block],
            dst_ref=held.at[1, slot, block],
            send_sem=pass_sem.at[slot, place_of(block)],
            recv_sem=recv_sem.at[1, slot, block],
            device_id=(layer, sibling),
            device_id_type=MESH,
        )

    def arrived(kind, slot, block):
        pltpu.make_async_copy(
            held.at[kind, slot, block], held.at[kind, slot, block], recv_sem.at[kind, slot, block]
        ).wait()

    def ways_of(slot, owner):
        wanted = jnp.logical_or(slot < steps, has_next)
        return (
            (LEFT, jnp.logical_and(wanted, jnp.logical_and(has_left, owner >= chip))),
            (RIGHT, jnp.logical_and(wanted, jnp.logical_and(has_right, owner <= chip))),
            (NEXT, jnp.logical_and(has_next, slot >= 1)),
            (SIBLING, slot < steps),
        )

    def send_hidden(slot, owner, block):
        for way, condition in ways_of(slot, owner):
            pl.when(condition)(lambda way=way: hidden_copy(slot, block, way).start())

    cell_ref[...] = c_start_ref[...]

    for part in range(cuts):
        start_copy(part).wait()
        send_hidden(0, chip, me * cuts + part)

    def multiply(kind, slot, block):
        rows = pl.ds(pl.multiple_of(block * piece, piece), piece)
        gates[...] += jnp.dot(
            held[kind, slot, block], weights[kind, rows, :], preferred_element_type=jnp.float32
        )

    def opening(index, _):
        away, passed, upward = index // 4, lax.rem(index // 2, 2), lax.rem(index, 2)
        owner = jnp.where(upward == 0, chip - away, chip + away)
        col = 2 * owner + jnp.where(passed == 0, core, 1 - core)
        valid = jnp.logical_and(owner >= 0, owner < chips)
        valid = jnp.logical_and(valid, jnp.logical_or(away > 0, upward == 0))
        valid = jnp.logical_and(valid, jnp.logical_or(away > 0, passed == 1))

        @pl.when(valid)
        def _():
            for part in range(cuts):
                block = col * cuts + part
                arrived(0, 0, block)
                pl.when(passed == 0)(lambda block=block: send_hidden(0, owner, block))

        unpack(index)

        @pl.when(jnp.logical_and(layer == 0, index >= devices))
        def _():
            @pl.loop(0, cuts)
            def _(part):
                ready = (index - devices) * cuts + part
                arrived(1, 0, ready)
                multiply(1, 0, ready)

        return 0

    gates[...] = jnp.broadcast_to(bias_ref[...], gates.shape)
    lax.fori_loop(0, chunks, opening, 0)

    def turn(slot, _):
        compute = slot < steps
        first = slot == 0
        half, whole = 4 * cuts * chips, 8 * cuts

        @pl.when(jnp.logical_and(compute, jnp.logical_not(first)))
        def _():
            gates[...] = jnp.broadcast_to(bias_ref[...], gates.shape)

        def event(index, _):
            place = jnp.where(first, lax.rem(index, half), index)
            away = jnp.where(first, place // (4 * cuts), place // whole)
            place = jnp.where(first, lax.rem(place, 4 * cuts), lax.rem(place, whole))
            kind = jnp.where(first, index // half, lax.rem(place // 2, 2))
            passed = jnp.where(first, place // (2 * cuts), place // (4 * cuts))
            part = jnp.where(first, lax.rem(place // 2, cuts), lax.rem(place // 4, cuts))
            upward = lax.rem(index, 2)
            late = jnp.logical_and(passed == 1, jnp.logical_not(first))
            away = jnp.where(late, away - 1, away)
            owner = jnp.where(upward == 0, chip - away, chip + away)
            block = (2 * owner + jnp.where(passed == 0, core, 1 - core)) * cuts + part
            valid = jnp.logical_and(owner >= 0, owner < chips)
            valid = jnp.logical_and(valid, jnp.logical_or(away > 0, upward == 0))
            valid = jnp.logical_and(
                valid, jnp.logical_or(compute, jnp.logical_and(kind == 0, passed == 0))
            )

            valid = jnp.logical_and(valid, jnp.logical_and(away >= 0, jnp.logical_or(index < 2 * half, jnp.logical_not(first))))
            ahead = jnp.logical_and(jnp.logical_and(layer == 0, first), kind == 1)
            valid = jnp.logical_and(valid, jnp.logical_not(ahead))

            @pl.when(valid)
            def _():
                mine = jnp.logical_and(away == 0, passed == 0)
                here = jnp.logical_and(kind == 0, jnp.logical_or(mine, first))

                @pl.when(jnp.logical_not(here))
                def _():
                    arrived(kind, slot, block)

                    @pl.when(jnp.logical_and(kind == 0, passed == 0))
                    def _():
                        send_hidden(slot, owner, block)

                    @pl.when(jnp.logical_and(kind == 1, jnp.logical_and(passed == 0, has_prev)))
                    def _():
                        source_copy(slot, block).start()

                @pl.when(compute)
                def _():
                    multiply(kind, slot, block)

            return 0

        lax.fori_loop(0, 8 * cuts * (chips + 1), event, 0)

        @pl.when(compute)
        def _():
            height = 32
            for part in range(cuts):
                columns = slice(part * piece, (part + 1) * piece)

                def rows_of(index, _):
                    rows = pl.ds(pl.multiple_of(index * height, height), height)

                    def gate(which):
                        return gates[
                            rows, which * local + part * piece : which * local + (part + 1) * piece
                        ]

                    cell = jax.nn.sigmoid(gate(1)) * cell_ref[rows, columns] + jax.nn.sigmoid(
                        gate(0)
                    ) * jnp.tanh(gate(2))
                    cell_ref[rows, columns] = cell
                    hidden = (jax.nn.sigmoid(gate(3)) * jnp.tanh(cell)).astype(jnp.bfloat16)
                    hidden_ref[slot, rows, columns] = hidden
                    held[0, slot + 1, me * cuts + part, rows, :] = hidden
                    return 0

                lax.fori_loop(0, batch // height, rows_of, 0)
                send_hidden(slot + 1, chip, me * cuts + part)

        return 0

    turns = jnp.where(has_next, steps + 1, steps)
    lax.fori_loop(0, turns, turn, 0)

    def drain(slot, _):
        def drain_block(index, _):
            owner, part = index // cuts, lax.rem(index, cuts)
            block = (2 * owner + core) * cuts + part
            for way, condition in ways_of(slot, owner):
                pl.when(condition)(lambda way=way: hidden_copy(slot, block, way).wait_send())

            @pl.when(jnp.logical_and(has_prev, slot < steps))
            def _():
                source_copy(slot, block).wait_send()

            return 0

        return lax.fori_loop(0, chips * cuts, drain_block, 0)

    lax.fori_loop(0, turns, drain, 0)


def body(inputs, w_input, w_recur, bias, h_start, c_start):
    steps, batch, width = inputs.shape
    local = w_input.shape[3]
    groups = lax.axis_size("layer")
    devices = lax.axis_size("col")
    cuts = 1
    vmem = pl.BlockSpec(memory_space=pltpu.VMEM)
    anywhere = pl.BlockSpec(memory_space=pl.ANY)
    hidden, cell = pl.pallas_call(
        functools.partial(kernel, groups, devices, cuts),
        out_shape=(
            jax.ShapeDtypeStruct((steps, batch, local), jnp.bfloat16),
            jax.ShapeDtypeStruct((batch, local), jnp.float32),
        ),
        in_specs=[anywhere, anywhere, anywhere, vmem, anywhere, vmem],
        out_specs=(vmem, vmem),
        scratch_shapes=[
            pltpu.VMEM((2, width, 4 * local), jnp.bfloat16),
            pltpu.VMEM((4, local, 4, local), jnp.bfloat16),
            pltpu.VMEM((2, steps + 1, devices * cuts, batch, local // cuts), jnp.bfloat16),
            pltpu.VMEM((batch, 4 * local), jnp.float32),
            pltpu.SemaphoreType.DMA((2, steps + 1, devices * cuts)),
            pltpu.SemaphoreType.DMA((steps + 1, devices // 2 * cuts, 4)),
            pltpu.SemaphoreType.DMA((steps, devices // 2 * cuts)),
            pltpu.SemaphoreType.DMA((4,)),
        ],
        compiler_params=pltpu.CompilerParams(
            collective_id=0, has_side_effects=True, vmem_limit_bytes=60 * 1024 * 1024
        ),
    )(
        inputs,
        w_input[0],
        w_recur[0],
        bias[0].reshape(1, 4 * local),
        h_start[0],
        c_start[0],
    )
    return (hidden[None], cell[None])


def solution(mesh):
    in_specs = (
        P(),
        P("layer", None, None, "col"),
        P("layer", None, None, "col"),
        P("layer", None, "col"),
        P("layer", None, "col"),
        P("layer", None, "col"),
    )
    out_specs = (P("layer", None, None, "col"), P("layer", None, "col"))
    return jax.shard_map(body, mesh=mesh, in_specs=in_specs, out_specs=out_specs, check_vma=False)
```
